256 devices in a mesh: grp: 4 (over x), box: 64 (over y, z, core).
Axes of the slice: x: 4, y: 4, z: 8, core: 2. Of those that a mesh axis runs over, the one named last changes fastest.
Arguments:
- source: float32 [128, 64, 16, 128], P('grp', 'box'), may hold values from -6 to 6
- alpha_coef: float32 [128, 64, 16, 128], P('grp', 'box'), may hold values from 0.02 to 0.2
- beta_coef: float32 [128, 64, 16, 128], P('grp', 'box'), may hold values from 0.5 to 5
Outputs:
- solution: float32 [128, 64, 16, 128], P('grp', 'box')
The draws below stay inside these ranges and needn't reach their ends.
All inputs are finite; a program needn't handle non-finite values.
Results may differ from the reference program's by a relative error of at most 0.00002.
Values sent between devices are 32-bit elements; how exact they have to be, the bound alone decides.
A program may use at most 128 MiB of HBM per device.

```python
import math
import jax
import jax.numpy as jnp
import numpy as np

CY = 16
NZ = 128
SWEEPS = 2
COARSE_SWEEPS = 4
NX = 128
NY = 1024
N_BOX = 64


def block_levels(own_key, dims, pieces, low, high):
    loudness = 1.0
    for axis_at, blocks in pieces:
        heights = jax.random.uniform(jax.random.fold_in(jax.random.fold_in(own_key, 6), axis_at), (blocks,), jnp.float32, low / len(pieces), high / len(pieces))
        loudness = loudness * jnp.repeat(jnp.exp(heights), dims[axis_at] // blocks).reshape((-1,) + (1,) * (len(dims) - 1 - axis_at))
    return loudness


def centred(own_key, shape, scale, reach, cuts=(), held_as=jnp.bfloat16):
    entries = jax.random.normal(own_key, shape, jnp.float32) * scale
    if len(cuts) > 0:
        entries = block_levels(own_key, shape, cuts, -0.22, 0.18) * entries
    return jnp.clip(entries, min=-reach, max=reach).astype(held_as)


def setup_inputs(seed: int = 0) -> dict:
    keys = jax.random.split(jax.random.key(seed), 4)
    return {
        "source": centred(keys[0], (NX, N_BOX, CY, NZ), 1.0, 6.0, ((0, 4), (1, 64)), jnp.float32),
        "alpha_coef": jnp.clip(jnp.exp(math.log(0.2) - 2.3025851 * jax.random.uniform(keys[1], (NX, N_BOX, CY, NZ), jnp.float32) ** block_levels(keys[1], (NX, N_BOX, CY, NZ), ((0, 4), (1, 64)), -0.2, 0.2)), 0.02, 0.2),
        "beta_coef": jnp.clip(jnp.exp(math.log(5.0) - 2.3025851 * jax.random.uniform(keys[2], (NX, N_BOX, CY, NZ), jnp.float32) ** block_levels(keys[2], (NX, N_BOX, CY, NZ), ((0, 4), (1, 64)), -0.2, 0.2)), 0.5, 5.0),
    }


OMEGA = 0.7
SHIFTS = ((1, 0, 0), (-1, 0, 0), (0, 1, 0), (0, -1, 0), (0, 0, 1), (0, 0, -1))


def inner_view(padded, step_x, step_y, step_z):
    return padded[1 + step_x:padded.shape[0] - 1 + step_x, 1 + step_y:padded.shape[1] - 1 + step_y, 1 + step_z:padded.shape[2] - 1 + step_z]


def neighbours(field_pad, beta_pad):
    centre = inner_view(beta_pad, 0, 0, 0)
    diag_sum = jnp.zeros(centre.shape, jnp.float32)
    off_sum = jnp.zeros(centre.shape, jnp.float32)
    for shift in SHIFTS:
        face_coef = 0.5 * (centre + inner_view(beta_pad, shift[0], shift[1], shift[2]))
        diag_sum = diag_sum + face_coef
        off_sum = off_sum + face_coef * inner_view(field_pad, shift[0], shift[1], shift[2])
    return diag_sum, off_sum


def applied_global(field, alpha_c, beta_c, scale):
    diag_sum, off_sum = neighbours(jnp.pad(field, 1), jnp.pad(beta_c, 1))
    return alpha_c * field + scale * (diag_sum * field - off_sum), diag_sum


def jacobi_global(field, source, alpha_c, beta_c, scale):
    applied, diag_sum = applied_global(field, alpha_c, beta_c, scale)
    return field + OMEGA * (source - applied) / (alpha_c + scale * diag_sum)


def restrict(values):
    shaped = values.reshape(values.shape[0] // 2, 2, values.shape[1] // 2, 2, values.shape[2] // 2, 2)
    return jnp.sum(shaped, axis=(1, 3, 5)) * 0.125


def prolong(coarse):
    wide = jnp.broadcast_to(coarse[:, None, :, None, :, None], (coarse.shape[0], 2, coarse.shape[1], 2, coarse.shape[2], 2))
    return wide.reshape(2 * coarse.shape[0], 2 * coarse.shape[1], 2 * coarse.shape[2])


def block_order():
    return np.array([slot_pos ^ (slot_pos >> 1) for slot_pos in range(N_BOX)], dtype=np.int32)


def to_grid(values):
    return values[:, block_order()].reshape(NX, NY, NZ)


def from_grid(values):
    inverse = np.argsort(block_order()).astype(np.int32)
    return values.reshape(NX, N_BOX, CY, NZ)[:, inverse]


def reference(source, alpha_coef, beta_coef):
    source = to_grid(source)
    alpha_coef = to_grid(alpha_coef)
    beta_coef = to_grid(beta_coef)
    field0 = jnp.zeros(source.shape, jnp.float32)
    for sweep in range(SWEEPS):
        field0 = jacobi_global(field0, source, alpha_coef, beta_coef, 1.0)
    applied, unused = applied_global(field0, alpha_coef, beta_coef, 1.0)
    source1 = restrict(source - applied)
    alpha1 = restrict(alpha_coef)
    beta1 = restrict(beta_coef)
    field1 = jnp.zeros(source1.shape, jnp.float32)
    for sweep in range(SWEEPS):
        field1 = jacobi_global(field1, source1, alpha1, beta1, 0.25)
    applied, unused = applied_global(field1, alpha1, beta1, 0.25)
    source2 = restrict(source1 - applied)
    alpha2 = restrict(alpha1)
    beta2 = restrict(beta1)
    field2 = jnp.zeros(source2.shape, jnp.float32)
    for sweep in range(COARSE_SWEEPS):
        field2 = jacobi_global(field2, source2, alpha2, beta2, 0.0625)
    field1 = field1 + prolong(field2)
    for sweep in range(SWEEPS):
        field1 = jacobi_global(field1, source1, alpha1, beta1, 0.25)
    field0 = field0 + prolong(field1)
    for sweep in range(SWEEPS):
        field0 = jacobi_global(field0, source, alpha_coef, beta_coef, 1.0)
    return from_grid(field0)
```

```python
import jax
import jax.numpy as jnp
from jax import lax
from jax.experimental import pallas as pl
from jax.experimental.pallas import tpu as pltpu
from jax.sharding import PartitionSpec as P

OMEGA = 0.7
F32 = jnp.float32
MESH = pl.DeviceIdType.MESH
LANES = 128

DIRECTIONS = [(dx, dp) for dx in (-1, 0, 1) for dp in (-2, -1, 0, 1, 2) if (dx, dp) != (0, 0)]
DIAGONALS = [(-1, -1), (-1, 1), (1, -1), (1, 1)]


class Level:
    def __init__(self, own_x, own_y, right, rows, off_y, stretch, scale):
        self.own_x, self.own_y, self.right, self.rows = own_x, own_y, right, rows
        self.off_y, self.stretch, self.scale = off_y, stretch, scale


L0 = Level(32, 16, 4, 40, 3, 1, 1.0)
L1 = Level(16, 8, 8, 32, 6, 2, 0.25)
L2 = Level(8, 4, 8, 24, 8, 4, 0.0625)

SCRATCH = {}
for name in ("nf", "na", "nb"):
    SCRATCH[name] = (640, LANES)
for name in ("ef", "ea", "eb", "w0", "x0", "v0"):
    SCRATCH[name] = (22, 40, LANES)
COEFS = ("cxp", "cxm", "cyp", "cym", "czp", "czm", "inv", "dia", "g")
for name in COEFS:
    SCRATCH[name + "0"] = (22, 40, LANES)
    SCRATCH[name + "1"] = (20, 32, LANES)
    SCRATCH[name + "2"] = (20, 24, LANES)
SCRATCH["syf"] = (2, 2, 32, LANES)
SCRATCH["sya"] = (2, 2, 32, LANES)
SCRATCH["syb"] = (2, 3, 32, LANES)
SCRATCH["sc"] = (4, 16, LANES)
SCRATCH["lc"] = (4, 16, LANES)
SCRATCH["lv"] = (2, 2, 40, LANES)
SCRATCH["rs0"] = (16, 32, LANES)
for name in ("p1f", "p1a", "p1b"):
    SCRATCH[name] = (10, 32, LANES)
for name in ("u1f", "u1a", "u1b", "v1", "w1", "x1"):
    SCRATCH[name] = (20, 32, LANES)
SCRATCH["rs1"] = (8, 16, LANES)
SCRATCH["p2c"] = (2, 5, 24, LANES)
SCRATCH["p2f"] = (5, 24, LANES)
for name in ("u2f", "u2a", "u2b", "w2", "x2"):
    SCRATCH[name] = (20, 24, LANES)
SCRATCH["t1"] = (8, 32, LANES)
SCRATCH["t0"] = (10, 40, LANES)
SCRATCH["out"] = (512, LANES)
N_MESSAGES = 64


def gray(place):
    return place ^ (place >> 1)


def each(low, high, step, work):
    count = (high - low) // step
    if count == 1:
        work(low)
    else:

        @pl.loop(0, count)
        def _(k):
            work(low + k * step)


def lane_index(shape):
    return lax.broadcasted_iota(jnp.int32, shape, len(shape) - 1)


def shift(values, axis, amount):
    size = values.shape[axis]
    return pltpu.roll(values, (-amount) % size, axis)


def pair_lanes(values, width):
    lanes = lane_index(values.shape)
    low_half = (lanes // width) % 2 == 0
    axis = values.ndim - 1
    return values + jnp.where(low_half, shift(values, axis, width), shift(values, axis, -width))


def pack2(even, odd):
    return jnp.where(lane_index(even.shape) % 2 == 0, even, odd)


def pack4(planes):
    lanes = lane_index(planes[0].shape) % 4
    packed = planes[3]
    for k in (2, 1, 0):
        packed = jnp.where(lanes == k, planes[k], packed)
    return packed


def unpack2(packed):
    even = lane_index(packed.shape) % 2 == 0
    axis = packed.ndim - 1
    return jnp.where(even, packed, shift(packed, axis, -1)), jnp.where(even, shift(packed, axis, 1), packed)


def unpack4(packed):
    lanes = lane_index(packed.shape) % 4
    axis = packed.ndim - 1
    moved = {d: (packed if d == 0 else shift(packed, axis, d)) for d in range(-3, 4)}
    planes = []
    for k in range(4):
        plane = moved[k - 3]
        for j in (2, 1, 0):
            plane = jnp.where(lanes == j, moved[k - j], plane)
        planes.append(plane)
    return planes


def make_kernel(groups, boxes):
    names = list(SCRATCH)

    def kernel(f_hbm, a_hbm, b_hbm, o_hbm, *scratch):
        r = dict(zip(names, scratch[: len(names)]))
        load_sem, store_sem, send_sem, recv_sem = scratch[len(names) :]
        gx = lax.axis_index("grp")
        code = lax.axis_index("box")
        pos = code
        for bits in range(1, (boxes - 1).bit_length()):
            pos = pos ^ (code >> bits)

        def exists(dx, dp):
            nx, npos = gx + dx, pos + dp
            return (nx >= 0) & (nx < groups) & (npos >= 0) & (npos < boxes)

        def device(dx, dp):
            nx = lax.rem(gx + dx + groups, groups)
            npos = lax.rem(pos + dp + boxes, boxes)
            return (nx, gray(npos))

        serial = [0]
        sent = []

        def message(direction, source, target):
            k = serial[0]
            serial[0] += 1
            copy = pltpu.make_async_remote_copy(
                src_ref=source,
                dst_ref=target,
                send_sem=send_sem.at[k],
                recv_sem=recv_sem.at[k],
                device_id=device(*direction),
                device_id_type=MESH,
            )
            return direction, copy

        def start(messages):
            for direction in dict.fromkeys(d for d, copy in messages):

                @pl.when(exists(*direction))
                def _():
                    for d, copy in messages:
                        if d == direction:
                            copy.start()

            sent.extend(messages)

        def arrive(messages):
            for direction in dict.fromkeys(d for d, copy in messages):

                @pl.when(exists(-direction[0], -direction[1]))
                def _():
                    for d, copy in messages:
                        if d == direction:
                            copy.wait_recv()

        loads = [
            pltpu.make_async_copy(hbm, r[name].at[pl.ds(0, 512)], load_sem.at[k])
            for k, (hbm, name) in enumerate(((b_hbm, "nb"), (f_hbm, "nf"), (a_hbm, "na")))
        ]
        for copy in loads:
            copy.start()

        def preset(ref, value):
            ref[...] = jnp.full(ref.shape, value, F32)

        for suffix, value in (("f", 0.0), ("a", 1.0), ("b", 0.0)):
            preset(r["n" + suffix].at[pl.ds(512, 128)], value)
            preset(r["e" + suffix].at[pl.ds(0, 3)], value)
            preset(r["e" + suffix].at[pl.ds(19, 3)], value)
            preset(r["p1" + suffix], value)
        corner_row = lax.broadcasted_iota(jnp.int32, (4, 16, LANES), 1)
        r["lc"][...] = jnp.where((corner_row >= 4) & (corner_row < 8), 1.0, 0.0).astype(F32)
        preset(r["lv"], 0.0)
        preset(r["p2f"], 0.0)
        preset(r["p2c"].at[0], 1.0)
        preset(r["p2c"].at[1], 0.0)

        barrier = pltpu.get_barrier_semaphore()
        expected = jnp.int32(0)
        for direction in DIRECTIONS:
            there = exists(*direction)
            expected = expected + there.astype(jnp.int32)

            @pl.when(there)
            def _():
                pl.semaphore_signal(barrier, inc=1, device_id=device(*direction), device_id_type=MESH)

        for copy in loads:
            copy.wait()

        for suffix, width in (("b", 3), ("f", 2), ("a", 2)):
            native, stage = r["n" + suffix], r["sy" + suffix]
            for k in range(width):
                stage[0, k] = native[pl.ds(16 - width + k, 32, stride=16), :]
                stage[1, k] = native[pl.ds(k, 32, stride=16), :]
        for d, (dx, dp) in enumerate(DIAGONALS):
            x = 28 if dx > 0 else 0
            near, far = (15, 14) if dp > 0 else (0, 1)
            for q, (name, y) in enumerate((("nf", near), ("na", near), ("nb", near), ("nb", far))):
                r["sc"][d, 4 * q : 4 * q + 4] = r[name][pl.ds(x * 16 + y, 4, stride=16), :]

        rim = []
        for dp in (-1, 1):
            side = 0 if dp > 0 else 1
            for suffix, width in (("b", 3), ("f", 2), ("a", 2)):
                at = 3 - width if dp > 0 else 19
                rim.append(
                    message(
                        (0, dp),
                        r["sy" + suffix].at[side],
                        r["e" + suffix].at[pl.ds(at, width), pl.ds(0, 32)],
                    )
                )
        for d, direction in enumerate(DIAGONALS):
            rim.append(message(direction, r["sc"].at[d], r["lc"].at[d]))
        rim_x = []
        for dx in (-1, 1):
            for suffix, hbm, width in (("b", b_hbm, 4), ("f", f_hbm, 3), ("a", a_hbm, 3)):
                if dx > 0:
                    source, target = 16 * (32 - width), 16 * (40 - width)
                else:
                    source, target = 0, 512
                rim_x.append(
                    message(
                        (dx, 0),
                        hbm.at[pl.ds(source, 16 * width)],
                        r["n" + suffix].at[pl.ds(target, 16 * width)],
                    )
                )
        pl.semaphore_wait(barrier, expected)
        start(rim)
        start(rim_x)

        for suffix in ("b", "a"):
            native, flat, packed = r["n" + suffix], r["u1" + suffix], r["p1" + suffix]
            for j in range(8):
                total = native[pl.ds(2 * j, 16, stride=32), :] + native[pl.ds(2 * j + 16, 16, stride=32), :]
                total = total + native[pl.ds(2 * j + 1, 16, stride=32), :]
                total = total + native[pl.ds(2 * j + 17, 16, stride=32), :]
                flat[6 + j, 0:16] = pair_lanes(total, 1) * 0.125
            for j in range(4):
                packed[3 + j, 0:16] = pack2(flat[6 + 2 * j, 0:16], flat[7 + 2 * j, 0:16])
            planes = []
            for j in range(4):
                total = flat[6 + 2 * j, pl.ds(0, 8, stride=2), :] + flat[6 + 2 * j, pl.ds(1, 8, stride=2), :]
                total = total + flat[7 + 2 * j, pl.ds(0, 8, stride=2), :]
                total = total + flat[7 + 2 * j, pl.ds(1, 8, stride=2), :]
                planes.append(pair_lanes(total, 2) * 0.125)
            r["p2c"][0 if suffix == "a" else 1, 2, 0:8] = pack4(planes)

        coarse_y = []
        for dp in (-1, 1):
            for name, width in (("p1b", 3), ("p1a", 2)):
                source = 7 - width if dp > 0 else 3
                target = 3 - width if dp > 0 else 7
                coarse_y.append(
                    message(
                        (0, dp),
                        r[name].at[pl.ds(source, width), pl.ds(0, 16)],
                        r[name].at[pl.ds(target, width), pl.ds(0, 16)],
                    )
                )
        for dp in (-2, -1, 1, 2):
            coarse_y.append(
                message(
                    (0, dp),
                    r["p2c"].at[:, 2, pl.ds(0, 8)],
                    r["p2c"].at[:, 2 - dp, pl.ds(0, 8)],
                )
            )
        start(coarse_y)

        def coefficients(level, tag, b, a, low, high, step, f=None):
            c = {name: r[name + tag] for name in COEFS}
            half = 0.5 * level.scale
            shape = (step, level.rows, LANES)
            lanes = lane_index(shape)
            keep_up = lanes < LANES - level.stretch
            keep_down = lanes >= level.stretch
            row = lax.broadcasted_iota(jnp.int32, shape, 1)
            row = jnp.where(row < level.own_x + level.right, row, row - level.rows) + gx * level.own_x
            row_ok = (row >= 0) & (row < groups * level.own_x)
            plane = lax.broadcasted_iota(jnp.int32, shape, 0)

            def work(i):
                here = pl.ds(i, step)
                centre = b[here]
                xp = half * (centre + shift(centre, 1, 1))
                xm = half * (centre + shift(centre, 1, -1))
                yp = half * (centre + b[pl.ds(i + 1, step)])
                ym = half * (centre + b[pl.ds(i - 1, step)])
                zp = half * (centre + jnp.where(keep_up, shift(centre, 2, level.stretch), 0.0))
                zm = half * (centre + jnp.where(keep_down, shift(centre, 2, -level.stretch), 0.0))
                diagonal = a[here] + (((xp + xm) + (yp + ym)) + (zp + zm))
                y = plane + (i - level.off_y + pos * level.own_y)
                ok = row_ok & (y >= 0) & (y < boxes * level.own_y)
                inverse = jnp.where(ok, OMEGA / diagonal, 0.0)
                c["cxp"][here] = xp
                c["cxm"][here] = xm
                c["cyp"][here] = yp
                c["cym"][here] = ym
                c["czp"][here] = jnp.where(keep_up, zp, 0.0)
                c["czm"][here] = jnp.where(keep_down, zm, 0.0)
                c["dia"][here] = diagonal
                c["inv"][here] = inverse
                if f is not None:
                    c["g"][here] = inverse * f[here]

            each(low, high, step, work)

        def spread(level, tag, field, i, step, rows=None):
            c = {name: r[name + tag] for name in COEFS}
            here = pl.ds(i, step)
            centre = field[here]
            up, down = field[pl.ds(i + 1, step)], field[pl.ds(i - 1, step)]
            cut = (lambda v: v) if rows is None else (lambda v: v[:, :rows])
            xs = c["cxp"][here] * shift(centre, 1, 1) + c["cxm"][here] * shift(centre, 1, -1)
            ys = c["cyp"][here] * up + c["cym"][here] * down
            zs = c["czp"][here] * shift(centre, 2, level.stretch) + c["czm"][here] * shift(centre, 2, -level.stretch)
            return cut(centre), cut(xs + ys + zs)

        def second_sweep(level, tag, target, low, high, step):
            def work(i):
                here = pl.ds(i, step)
                centre, total = spread(level, tag, r["g" + tag], i, step)
                target[here] = 1.3 * centre + r["inv" + tag][here] * total

            each(low, high, step, work)

        def sweep(level, tag, field, target, low, high, step):
            def work(i):
                here = pl.ds(i, step)
                centre, total = spread(level, tag, field, i, step)
                target[here] = (0.3 * centre + r["g" + tag][here]) + r["inv" + tag][here] * total

            each(low, high, step, work)

        def residual(level, tag, field, f, target, low, high, step):
            rows = level.own_x

            def work(i):
                here = pl.ds(i, step)
                centre, total = spread(level, tag, field, i, step, rows)
                target[pl.ds(i - level.off_y, step)] = f[here, 0:rows] - r["dia" + tag][here, 0:rows] * centre + total

            each(low, high, step, work)

        def restrict_plane(source, j, rows, width):
            half = rows // 2
            total = source[2 * j, pl.ds(0, half, stride=2), :] + source[2 * j, pl.ds(1, half, stride=2), :]
            total = total + source[2 * j + 1, pl.ds(0, half, stride=2), :]
            total = total + source[2 * j + 1, pl.ds(1, half, stride=2), :]
            return pair_lanes(total, width) * 0.125

        def restrict_pairs(pairs):
            for k in pairs:
                even = restrict_plane(r["rs0"], 2 * k, 32, 1)
                odd = restrict_plane(r["rs0"], 2 * k + 1, 32, 1)
                r["u1f"][6 + 2 * k, 0:16] = even
                r["u1f"][7 + 2 * k, 0:16] = odd
                r["p1f"][3 + k, 0:16] = pack2(even, odd)

        arrive(rim_x)

        def transpose(y):
            for suffix in ("f", "a", "b"):
                r["e" + suffix][y + 3] = r["n" + suffix][pl.ds(y, 40, stride=16), :]

        each(0, 16, 1, transpose)
        coefficients(L0, "0", r["eb"], r["ea"], 4, 18, 2, r["ef"])
        second_sweep(L0, "0", r["v0"], 5, 17, 3)
        residual(L0, "0", r["v0"], r["ef"], r["rs0"], 6, 16, 2)
        restrict_pairs((1, 2))

        arrive(rim)
        for d, (dx, dp) in enumerate(DIAGONALS):
            row = 36 if dx > 0 else 32
            near, far = (2, 1) if dp > 0 else (19, 20)
            for q, (name, y) in enumerate((("ef", near), ("ea", near), ("eb", near), ("eb", far))):
                r[name][y, row : row + 4] = r["lc"][d, 4 * q : 4 * q + 4]
        coefficients(L0, "0", r["eb"], r["ea"], 1, 4, 3, r["ef"])
        coefficients(L0, "0", r["eb"], r["ea"], 18, 21, 3, r["ef"])
        second_sweep(L0, "0", r["v0"], 2, 5, 3)
        second_sweep(L0, "0", r["v0"], 17, 20, 3)
        residual(L0, "0", r["v0"], r["ef"], r["rs0"], 3, 6, 3)
        residual(L0, "0", r["v0"], r["ef"], r["rs0"], 16, 19, 3)
        restrict_pairs((0, 3))

        second = []
        for dx in (-1, 0, 1):
            for dp in (-1, 0, 1):
                if (dx, dp) == (0, 0):
                    continue
                planes = (5, 2, 1) if dp > 0 else ((3, 2, 7) if dp < 0 else (3, 4, 3))
                rows = (8, 8, 24) if dx > 0 else ((0, 8, 16) if dx < 0 else (0, 16, 0))
                second.append(
                    message(
                        (dx, dp),
                        r["p1f"].at[pl.ds(planes[0], planes[1]), pl.ds(rows[0], rows[1])],
                        r["p1f"].at[pl.ds(planes[2], planes[1]), pl.ds(rows[2], rows[1])],
                    )
                )
        start(second)
        fine = [
            message((0, 1), r["v0"].at[pl.ds(17, 2)], r["lv"].at[0]),
            message((0, -1), r["v0"].at[pl.ds(3, 2)], r["lv"].at[1]),
        ]
        start(fine)

        arrive(coarse_y)
        coarse_x = []
        for dx in (-1, 1):
            source, target = (8, 24) if dx > 0 else (0, 16)
            for name, low, count in (("p1b", 0, 10), ("p1a", 1, 8)):
                coarse_x.append(
                    message(
                        (dx, 0),
                        r[name].at[pl.ds(low, count), pl.ds(source, 8)],
                        r[name].at[pl.ds(low, count), pl.ds(target, 8)],
                    )
                )
            coarse_x.append(
                message(
                    (dx, 0),
                    r["p2c"].at[:, :, pl.ds(0, 8)],
                    r["p2c"].at[:, :, pl.ds(16 if dx > 0 else 8, 8)],
                )
            )
        start(coarse_x)
        arrive(coarse_x)

        def unpack_pairs(packed, flat, low, high):
            def work(k):
                even, odd = unpack2(packed[k])
                flat[2 * k] = even
                flat[2 * k + 1] = odd

            each(low, high, 1, work)

        def unpack_quads(packed, flat):
            def work(k):
                for j, plane in enumerate(unpack4(packed[k])):
                    flat[4 * k + j] = plane

            each(0, 5, 1, work)

        unpack_pairs(r["p1b"], r["u1b"], 0, 10)
        unpack_pairs(r["p1a"], r["u1a"], 1, 9)
        coefficients(L1, "1", r["u1b"], r["u1a"], 2, 18, 4)
        unpack_quads(r["p2c"].at[0], r["u2a"])
        unpack_quads(r["p2c"].at[1], r["u2b"])
        coefficients(L2, "2", r["u2b"], r["u2a"], 3, 17, 7)

        arrive(second)
        unpack_pairs(r["p1f"], r["u1f"], 1, 9)

        def first_sweep(tag, f, low, high, step):
            def work(i):
                here = pl.ds(i, step)
                r["g" + tag][here] = r["inv" + tag][here] * f[here]

            each(low, high, step, work)

        first_sweep("1", r["u1f"], 2, 18, 8)
        second_sweep(L1, "1", r["v1"], 3, 17, 7)
        residual(L1, "1", r["v1"], r["u1f"], r["rs1"], 6, 14, 4)
        r["p2f"][2, 0:8] = pack4([restrict_plane(r["rs1"], j, 16, 2) for j in range(4)])

        third = []
        for dx, dp in DIRECTIONS:
            row = 16 if dx > 0 else (8 if dx < 0 else 0)
            third.append(
                message((dx, dp), r["p2f"].at[2, pl.ds(0, 8)], r["p2f"].at[2 - dp, pl.ds(row, 8)])
            )
        start(third)
        arrive(third)

        unpack_quads(r["p2f"], r["u2f"])
        first_sweep("2", r["u2f"], 3, 17, 7)
        second_sweep(L2, "2", r["w2"], 4, 16, 6)
        sweep(L2, "2", r["w2"], r["x2"], 5, 15, 5)
        sweep(L2, "2", r["x2"], r["w2"], 6, 14, 4)

        for q in range(6, 14):
            for half in (0, 1):
                r["t1"][q - 6, pl.ds(half, 12, stride=2), :] = r["w2"][q, 0:12]
                r["t1"][q - 6, pl.ds(24 + half, 4, stride=2), :] = r["w2"][q, 20:24]
            for half in (0, 1):
                i = 2 * q - 10 + half
                r["w1"][i] = r["v1"][i] + r["t1"][q - 6]
        sweep(L1, "1", r["w1"], r["x1"], 4, 16, 6)
        sweep(L1, "1", r["x1"], r["w1"], 5, 15, 5)

        arrive(fine)
        for q in range(5, 15):
            for half in (0, 1):
                r["t0"][q - 5, pl.ds(half, 18, stride=2), :] = r["w1"][q, 0:18]
                r["t0"][q - 5, pl.ds(36 + half, 2, stride=2), :] = r["w1"][q, 30:32]
            for half in (0, 1):
                i = 2 * q - 9 + half
                if q == 5:
                    before = r["lv"][0, half]
                elif q == 14:
                    before = r["lv"][1, half]
                else:
                    before = r["v0"][i]
                r["w0"][i] = before + r["t0"][q - 5]
        sweep(L0, "0", r["w0"], r["x0"], 2, 20, 3)

        def last(i):
            centre, total = spread(L0, "0", r["x0"], i, 2)
            here = pl.ds(i, 2)
            value = (0.3 * centre + r["g0"][here]) + r["inv0"][here] * total
            for k in range(2):
                r["out"][pl.ds(i - 3 + k, 32, stride=16), :] = value[k, 0:32]

        each(3, 19, 2, last)
        store = pltpu.make_async_copy(r["out"], o_hbm, store_sem)
        store.start()
        for direction in dict.fromkeys(d for d, copy in sent):

            @pl.when(exists(*direction))
            def _():
                for d, copy in sent:
                    if d == direction:
                        copy.wait_send()

        store.wait()
        assert serial[0] <= N_MESSAGES

    return kernel


def solution(mesh):
    groups, boxes = mesh.shape["grp"], mesh.shape["box"]

    def body(source, alpha_coef, beta_coef):
        flat = [v.reshape(512, LANES) for v in (source, alpha_coef, beta_coef)]
        hbm = pl.BlockSpec(memory_space=pl.ANY)
        out = pl.pallas_call(
            make_kernel(groups, boxes),
            out_shape=jax.ShapeDtypeStruct((512, LANES), F32),
            in_specs=[hbm, hbm, hbm],
            out_specs=hbm,
            scratch_shapes=[pltpu.VMEM(shape, F32) for shape in SCRATCH.values()]
            + [
                pltpu.SemaphoreType.DMA((3,)),
                pltpu.SemaphoreType.DMA,
                pltpu.SemaphoreType.DMA((N_MESSAGES,)),
                pltpu.SemaphoreType.DMA((N_MESSAGES,)),
            ],
            compiler_params=pltpu.CompilerParams(
                collective_id=0, has_side_effects=True, vmem_limit_bytes=48 * 1024 * 1024
            ),
        )(*flat)
        return out.reshape(32, 1, 16, LANES)

    spec = P("grp", "box", None, None)
    return jax.shard_map(body, mesh=mesh, in_specs=(spec, spec, spec), out_specs=spec, check_vma=False)
```

```python
import jax
import jax.numpy as jnp
from jax import lax
from jax.experimental import pallas as pl
from jax.experimental.pallas import tpu as pltpu
from jax.sharding import PartitionSpec as P

OMEGA = 0.7
F32 = jnp.float32
MESH = pl.DeviceIdType.MESH
LANES = 128

DIRECTIONS = [(dx, dp) for dx in (-1, 0, 1) for dp in (-2, -1, 0, 1, 2) if (dx, dp) != (0, 0)]
DIRECT = [(0, 1), (0, -1), (1, 0), (-1, 0)]
DIAGONALS = [(-1, -1), (-1, 1), (1, -1), (1, 1)]


class Level:
    def __init__(self, own_x, own_y, right, rows, off_y, stretch, scale):
        self.own_x, self.own_y, self.right, self.rows = own_x, own_y, right, rows
        self.off_y, self.stretch, self.scale = off_y, stretch, scale


L0 = Level(32, 16, 4, 40, 3, 1, 1.0)
L1 = Level(16, 8, 8, 32, 6, 2, 0.25)
L2 = Level(8, 4, 8, 24, 8, 4, 0.0625)

SCRATCH = {}
for name in ("nf", "na", "nb"):
    SCRATCH[name] = (640, LANES)
for name in ("ef", "ea", "eb", "w0", "x0", "v0"):
    SCRATCH[name] = (22, 40, LANES)
COEFS = ("cxp", "cxm", "cyp", "cym", "czp", "czm", "inv", "dia", "g")
for name in COEFS:
    SCRATCH[name + "0"] = (22, 40, LANES)
    SCRATCH[name + "1"] = (20, 32, LANES)
    SCRATCH[name + "2"] = (20, 24, LANES)
SCRATCH["syf"] = (2, 2, 32, LANES)
SCRATCH["sya"] = (2, 2, 32, LANES)
SCRATCH["syb"] = (2, 3, 32, LANES)
SCRATCH["sc"] = (4, 16, LANES)
SCRATCH["lc"] = (4, 16, LANES)
SCRATCH["lv"] = (2, 2, 40, LANES)
SCRATCH["rs0"] = (16, 32, LANES)
for name in ("p1f", "p1a", "p1b"):
    SCRATCH[name] = (10, 32, LANES)
for name in ("u1f", "u1a", "u1b", "v1", "w1", "x1"):
    SCRATCH[name] = (20, 32, LANES)
SCRATCH["rs1"] = (8, 16, LANES)
SCRATCH["p2c"] = (2, 5, 24, LANES)
SCRATCH["p2f"] = (5, 24, LANES)
for name in ("u2f", "u2a", "u2b", "w2", "x2"):
    SCRATCH[name] = (20, 24, LANES)
SCRATCH["t1"] = (8, 32, LANES)
SCRATCH["t0"] = (10, 40, LANES)
N_MESSAGES = 64


def gray(place):
    return place ^ (place >> 1)


def each(low, high, step, work):
    count = (high - low) // step
    if count == 1:
        work(low)
    else:

        @pl.loop(0, count)
        def _(k):
            work(low + k * step)


def lane_index(shape):
    return lax.broadcasted_iota(jnp.int32, shape, len(shape) - 1)


def shift(values, axis, amount):
    size = values.shape[axis]
    return pltpu.roll(values, (-amount) % size, axis)


def pair_lanes(values, width):
    lanes = lane_index(values.shape)
    low_half = (lanes // width) % 2 == 0
    axis = values.ndim - 1
    return values + jnp.where(low_half, shift(values, axis, width), shift(values, axis, -width))


def pack2(even, odd):
    return jnp.where(lane_index(even.shape) % 2 == 0, even, odd)


def pack4(planes):
    lanes = lane_index(planes[0].shape) % 4
    packed = planes[3]
    for k in (2, 1, 0):
        packed = jnp.where(lanes == k, planes[k], packed)
    return packed


def unpack2(packed):
    even = lane_index(packed.shape) % 2 == 0
    axis = packed.ndim - 1
    return jnp.where(even, packed, shift(packed, axis, -1)), jnp.where(even, shift(packed, axis, 1), packed)


def unpack4(packed):
    lanes = lane_index(packed.shape) % 4
    axis = packed.ndim - 1
    moved = {d: (packed if d == 0 else shift(packed, axis, d)) for d in range(-3, 4)}
    planes = []
    for k in range(4):
        plane = moved[k - 3]
        for j in (2, 1, 0):
            plane = jnp.where(lanes == j, moved[k - j], plane)
        planes.append(plane)
    return planes


def make_kernel(groups, boxes):
    names = list(SCRATCH)

    def kernel(f_hbm, a_hbm, b_hbm, o_ref, *scratch):
        r = dict(zip(names, scratch[: len(names)]))
        load_sem, ready_sem, send_sem, recv_sem = scratch[len(names) :]
        gx = lax.axis_index("grp")
        code = lax.axis_index("box")
        pos = code
        for bits in range(1, (boxes - 1).bit_length()):
            pos = pos ^ (code >> bits)

        def exists(dx, dp):
            nx, npos = gx + dx, pos + dp
            return (nx >= 0) & (nx < groups) & (npos >= 0) & (npos < boxes)

        def device(dx, dp):
            nx = lax.rem(gx + dx + groups, groups)
            npos = lax.rem(pos + dp + boxes, boxes)
            return (nx, gray(npos))

        serial = [0]
        sent = []

        def message(direction, source, target):
            k = serial[0]
            serial[0] += 1
            copy = pltpu.make_async_remote_copy(
                src_ref=source,
                dst_ref=target,
                send_sem=send_sem.at[k],
                recv_sem=recv_sem.at[k],
                device_id=device(*direction),
                device_id_type=MESH,
            )
            return direction, copy

        def start(messages):
            for direction in dict.fromkeys(d for d, copy in messages):

                @pl.when(exists(*direction))
                def _():
                    for d, copy in messages:
                        if d == direction:
                            copy.start()

            sent.extend(messages)

        def arrive(messages):
            for direction in dict.fromkeys(d for d, copy in messages):

                @pl.when(exists(-direction[0], -direction[1]))
                def _():
                    for d, copy in messages:
                        if d == direction:
                            copy.wait_recv()

        loads = [
            pltpu.make_async_copy(hbm, r[name].at[pl.ds(0, 512)], load_sem.at[k])
            for k, (hbm, name) in enumerate(((b_hbm, "nb"), (f_hbm, "nf"), (a_hbm, "na")))
        ]
        for copy in loads:
            copy.start()

        def preset(ref, value):
            ref[...] = jnp.full(ref.shape, value, F32)

        for suffix, value in (("f", 0.0), ("a", 1.0), ("b", 0.0)):
            preset(r["n" + suffix].at[pl.ds(512, 128)], value)
            preset(r["e" + suffix].at[pl.ds(0, 3)], value)
            preset(r["e" + suffix].at[pl.ds(19, 3)], value)
            preset(r["p1" + suffix], value)
        corner_row = lax.broadcasted_iota(jnp.int32, (4, 16, LANES), 1)
        r["lc"][...] = jnp.where((corner_row >= 4) & (corner_row < 8), 1.0, 0.0).astype(F32)
        preset(r["lv"], 0.0)
        preset(r["p2f"], 0.0)
        preset(r["p2c"].at[0], 1.0)
        preset(r["p2c"].at[1], 0.0)

        barrier = pltpu.get_barrier_semaphore()
        expected = jnp.int32(0)
        for direction in DIRECT:
            there = exists(*direction)
            expected = expected + there.astype(jnp.int32)

            @pl.when(there)
            def _():
                pl.semaphore_signal(barrier, inc=1, device_id=device(*direction), device_id_type=MESH)

        for copy in loads:
            copy.wait()

        for suffix, width in (("b", 3), ("f", 2), ("a", 2)):
            native, stage = r["n" + suffix], r["sy" + suffix]
            for k in range(width):
                stage[0, k] = native[pl.ds(16 - width + k, 32, stride=16), :]
                stage[1, k] = native[pl.ds(k, 32, stride=16), :]
        for d, (dx, dp) in enumerate(DIAGONALS):
            x = 28 if dx > 0 else 0
            near, far = (15, 14) if dp > 0 else (0, 1)
            for q, (name, y) in enumerate((("nf", near), ("na", near), ("nb", near), ("nb", far))):
                r["sc"][d, 4 * q : 4 * q + 4] = r[name][pl.ds(x * 16 + y, 4, stride=16), :]

        rim = []
        for dp in (-1, 1):
            side = 0 if dp > 0 else 1
            for suffix, width in (("b", 3), ("f", 2), ("a", 2)):
                at = 3 - width if dp > 0 else 19
                rim.append(
                    message(
                        (0, dp),
                        r["sy" + suffix].at[side],
                        r["e" + suffix].at[pl.ds(at, width), pl.ds(0, 32)],
                    )
                )
        corners = [message(direction, r["sc"].at[d], r["lc"].at[d]) for d, direction in enumerate(DIAGONALS)]
        rim_x = []
        for dx in (-1, 1):
            for suffix, hbm, width in (("b", b_hbm, 4), ("f", f_hbm, 3), ("a", a_hbm, 3)):
                if dx > 0:
                    source, target = 16 * (32 - width), 16 * (40 - width)
                else:
                    source, target = 0, 512
                rim_x.append(
                    message(
                        (dx, 0),
                        hbm.at[pl.ds(source, 16 * width)],
                        r["n" + suffix].at[pl.ds(target, 16 * width)],
                    )
                )
        pl.semaphore_wait(barrier, expected)
        start(rim)
        for dx in (-1, 1):

            @pl.when(exists(dx, 0))
            def _():
                pl.semaphore_signal(ready_sem, inc=1, device_id=device(dx, 0), device_id_type=MESH)

        start(rim_x)
        pl.semaphore_wait(ready_sem, exists(-1, 0).astype(jnp.int32) + exists(1, 0).astype(jnp.int32))
        start(corners)

        for suffix in ("b", "a"):
            native, flat, packed = r["n" + suffix], r["u1" + suffix], r["p1" + suffix]
            for j in range(8):
                total = native[pl.ds(2 * j, 16, stride=32), :] + native[pl.ds(2 * j + 16, 16, stride=32), :]
                total = total + native[pl.ds(2 * j + 1, 16, stride=32), :]
                total = total + native[pl.ds(2 * j + 17, 16, stride=32), :]
                flat[6 + j, 0:16] = pair_lanes(total, 1) * 0.125
            for j in range(4):
                packed[3 + j, 0:16] = pack2(flat[6 + 2 * j, 0:16], flat[7 + 2 * j, 0:16])
            planes = []
            for j in range(4):
                total = flat[6 + 2 * j, pl.ds(0, 8, stride=2), :] + flat[6 + 2 * j, pl.ds(1, 8, stride=2), :]
                total = total + flat[7 + 2 * j, pl.ds(0, 8, stride=2), :]
                total = total + flat[7 + 2 * j, pl.ds(1, 8, stride=2), :]
                planes.append(pair_lanes(total, 2) * 0.125)
            r["p2c"][0 if suffix == "a" else 1, 2, 0:8] = pack4(planes)

        coarse_y = []
        for dp in (-1, 1):
            for name, width in (("p1b", 3), ("p1a", 2)):
                source = 7 - width if dp > 0 else 3
                target = 3 - width if dp > 0 else 7
                coarse_y.append(
                    message(
                        (0, dp),
                        r[name].at[pl.ds(source, width), pl.ds(0, 16)],
                        r[name].at[pl.ds(target, width), pl.ds(0, 16)],
                    )
                )
        coarsest_y = [
            message((0, dp), r["p2c"].at[:, 2, pl.ds(0, 8)], r["p2c"].at[:, 2 - dp, pl.ds(0, 8)])
            for dp in (-2, -1, 1, 2)
        ]
        start(coarse_y)

        def coefficients(level, tag, b, a, low, high, step, f=None):
            c = {name: r[name + tag] for name in COEFS}
            half = 0.5 * level.scale
            shape = (step, level.rows, LANES)
            lanes = lane_index(shape)
            keep_up = lanes < LANES - level.stretch
            keep_down = lanes >= level.stretch
            row = lax.broadcasted_iota(jnp.int32, shape, 1)
            row = jnp.where(row < level.own_x + level.right, row, row - level.rows) + gx * level.own_x
            row_ok = (row >= 0) & (row < groups * level.own_x)
            plane = lax.broadcasted_iota(jnp.int32, shape, 0)

            def work(i):
                here = pl.ds(i, step)
                centre = b[here]
                xp = half * (centre + shift(centre, 1, 1))
                xm = half * (centre + shift(centre, 1, -1))
                yp = half * (centre + b[pl.ds(i + 1, step)])
                ym = half * (centre + b[pl.ds(i - 1, step)])
                zp = half * (centre + jnp.where(keep_up, shift(centre, 2, level.stretch), 0.0))
                zm = half * (centre + jnp.where(keep_down, shift(centre, 2, -level.stretch), 0.0))
                diagonal = a[here] + (((xp + xm) + (yp + ym)) + (zp + zm))
                y = plane + (i - level.off_y + pos * level.own_y)
                ok = row_ok & (y >= 0) & (y < boxes * level.own_y)
                inverse = jnp.where(ok, OMEGA / diagonal, 0.0)
                c["cxp"][here] = xp
                c["cxm"][here] = xm
                c["cyp"][here] = yp
                c["cym"][here] = ym
                c["czp"][here] = jnp.where(keep_up, zp, 0.0)
                c["czm"][here] = jnp.where(keep_down, zm, 0.0)
                c["dia"][here] = diagonal
                c["inv"][here] = inverse
                if f is not None:
                    c["g"][here] = inverse * f[here]

            each(low, high, step, work)

        def spread(level, tag, field, i, step, rows=None):
            c = {name: r[name + tag] for name in COEFS}
            here = pl.ds(i, step)
            centre = field[here]
            up, down = field[pl.ds(i + 1, step)], field[pl.ds(i - 1, step)]
            cut = (lambda v: v) if rows is None else (lambda v: v[:, :rows])
            xs = c["cxp"][here] * shift(centre, 1, 1) + c["cxm"][here] * shift(centre, 1, -1)
            ys = c["cyp"][here] * up + c["cym"][here] * down
            zs = c["czp"][here] * shift(centre, 2, level.stretch) + c["czm"][here] * shift(centre, 2, -level.stretch)
            return cut(centre), cut(xs + ys + zs)

        def second_sweep(level, tag, target, low, high, step):
            def work(i):
                here = pl.ds(i, step)
                centre, total = spread(level, tag, r["g" + tag], i, step)
                target[here] = 1.3 * centre + r["inv" + tag][here] * total

            each(low, high, step, work)

        def sweep(level, tag, field, target, low, high, step):
            def work(i):
                here = pl.ds(i, step)
                centre, total = spread(level, tag, field, i, step)
                target[here] = (0.3 * centre + r["g" + tag][here]) + r["inv" + tag][here] * total

            each(low, high, step, work)

        def residual(level, tag, field, f, target, low, high, step):
            rows = level.own_x

            def work(i):
                here = pl.ds(i, step)
                centre, total = spread(level, tag, field, i, step, rows)
                target[pl.ds(i - level.off_y, step)] = f[here, 0:rows] - r["dia" + tag][here, 0:rows] * centre + total

            each(low, high, step, work)

        def restrict_plane(source, j, rows, width):
            half = rows // 2
            total = source[2 * j, pl.ds(0, half, stride=2), :] + source[2 * j, pl.ds(1, half, stride=2), :]
            total = total + source[2 * j + 1, pl.ds(0, half, stride=2), :]
            total = total + source[2 * j + 1, pl.ds(1, half, stride=2), :]
            return pair_lanes(total, width) * 0.125

        def restrict_pairs(pairs):
            for k in pairs:
                even = restrict_plane(r["rs0"], 2 * k, 32, 1)
                odd = restrict_plane(r["rs0"], 2 * k + 1, 32, 1)
                r["u1f"][6 + 2 * k, 0:16] = even
                r["u1f"][7 + 2 * k, 0:16] = odd
                r["p1f"][3 + k, 0:16] = pack2(even, odd)

        arrive(rim_x)

        def transpose(y):
            for suffix in ("f", "a", "b"):
                r["e" + suffix][y + 3] = r["n" + suffix][pl.ds(y, 40, stride=16), :]

        each(0, 16, 4, lambda y: [transpose(y + n) for n in range(4)])
        coefficients(L0, "0", r["eb"], r["ea"], 4, 18, 2, r["ef"])
        second_sweep(L0, "0", r["v0"], 5, 17, 3)
        residual(L0, "0", r["v0"], r["ef"], r["rs0"], 6, 16, 2)
        restrict_pairs((1, 2))

        arrive(rim)
        arrive(corners)
        start(coarsest_y)
        for d, (dx, dp) in enumerate(DIAGONALS):
            row = 36 if dx > 0 else 32
            near, far = (2, 1) if dp > 0 else (19, 20)
            for q, (name, y) in enumerate((("ef", near), ("ea", near), ("eb", near), ("eb", far))):
                r[name][y, row : row + 4] = r["lc"][d, 4 * q : 4 * q + 4]
        coefficients(L0, "0", r["eb"], r["ea"], 1, 4, 3, r["ef"])
        coefficients(L0, "0", r["eb"], r["ea"], 18, 21, 3, r["ef"])
        second_sweep(L0, "0", r["v0"], 2, 5, 3)
        second_sweep(L0, "0", r["v0"], 17, 20, 3)
        residual(L0, "0", r["v0"], r["ef"], r["rs0"], 3, 6, 3)
        residual(L0, "0", r["v0"], r["ef"], r["rs0"], 16, 19, 3)
        restrict_pairs((0, 3))

        second = []
        for dx in (-1, 0, 1):
            for dp in (-1, 0, 1):
                if (dx, dp) == (0, 0):
                    continue
                planes = (5, 2, 1) if dp > 0 else ((3, 2, 7) if dp < 0 else (3, 4, 3))
                rows = (8, 8, 24) if dx > 0 else ((0, 8, 16) if dx < 0 else (0, 16, 0))
                second.append(
                    message(
                        (dx, dp),
                        r["p1f"].at[pl.ds(planes[0], planes[1]), pl.ds(rows[0], rows[1])],
                        r["p1f"].at[pl.ds(planes[2], planes[1]), pl.ds(rows[2], rows[1])],
                    )
                )
        start(second)
        fine = [
            message((0, 1), r["v0"].at[pl.ds(17, 2)], r["lv"].at[0]),
            message((0, -1), r["v0"].at[pl.ds(3, 2)], r["lv"].at[1]),
        ]
        start(fine)

        arrive(coarse_y)
        coarse_x = []
        for dx in (-1, 1):
            source, target = (8, 24) if dx > 0 else (0, 16)
            for name, low, count in (("p1b", 0, 10), ("p1a", 1, 8)):
                coarse_x.append(
                    message(
                        (dx, 0),
                        r[name].at[pl.ds(low, count), pl.ds(source, 8)],
                        r[name].at[pl.ds(low, count), pl.ds(target, 8)],
                    )
                )
        coarsest_x = [
            message(
                (dx, 0),
                r["p2c"].at[:, :, pl.ds(0, 8)],
                r["p2c"].at[:, :, pl.ds(16 if dx > 0 else 8, 8)],
            )
            for dx in (-1, 1)
        ]
        start(coarse_x)
        arrive(coarse_x)

        def unpack_pairs(packed, flat, low, high):
            def work(k):
                even, odd = unpack2(packed[k])
                flat[2 * k] = even
                flat[2 * k + 1] = odd

            each(low, high, 2 if high - low == 10 else 4, lambda k: [work(k + n) for n in range(2 if high - low == 10 else 4)])

        def unpack_quads(packed, flat):
            def work(k):
                for j, plane in enumerate(unpack4(packed[k])):
                    flat[4 * k + j] = plane

            each(0, 5, 5, lambda k: [work(k + n) for n in range(5)])

        unpack_pairs(r["p1b"], r["u1b"], 0, 10)
        unpack_pairs(r["p1a"], r["u1a"], 1, 9)
        coefficients(L1, "1", r["u1b"], r["u1a"], 2, 18, 4)

        arrive(second)
        unpack_pairs(r["p1f"], r["u1f"], 1, 9)

        def first_sweep(tag, f, low, high, step):
            def work(i):
                here = pl.ds(i, step)
                r["g" + tag][here] = r["inv" + tag][here] * f[here]

            each(low, high, step, work)

        first_sweep("1", r["u1f"], 2, 18, 16)
        second_sweep(L1, "1", r["v1"], 3, 17, 14)
        residual(L1, "1", r["v1"], r["u1f"], r["rs1"], 6, 14, 8)
        r["p2f"][2, 0:8] = pack4([restrict_plane(r["rs1"], j, 16, 2) for j in range(4)])

        third = []
        for dx, dp in DIRECTIONS:
            row = 16 if dx > 0 else (8 if dx < 0 else 0)
            third.append(
                message((dx, dp), r["p2f"].at[2, pl.ds(0, 8)], r["p2f"].at[2 - dp, pl.ds(row, 8)])
            )
        start(third)
        arrive(coarsest_y)
        start(coarsest_x)
        arrive(coarsest_x)
        unpack_quads(r["p2c"].at[0], r["u2a"])
        unpack_quads(r["p2c"].at[1], r["u2b"])
        coefficients(L2, "2", r["u2b"], r["u2a"], 3, 17, 7)
        arrive(third)

        unpack_quads(r["p2f"], r["u2f"])
        first_sweep("2", r["u2f"], 3, 17, 14)
        second_sweep(L2, "2", r["w2"], 4, 16, 12)
        sweep(L2, "2", r["w2"], r["x2"], 5, 15, 10)
        sweep(L2, "2", r["x2"], r["w2"], 6, 14, 8)

        for q in range(6, 14):
            for half in (0, 1):
                r["t1"][q - 6, pl.ds(half, 12, stride=2), :] = r["w2"][q, 0:12]
                r["t1"][q - 6, pl.ds(24 + half, 4, stride=2), :] = r["w2"][q, 20:24]
            for half in (0, 1):
                i = 2 * q - 10 + half
                r["w1"][i] = r["v1"][i] + r["t1"][q - 6]
        sweep(L1, "1", r["w1"], r["x1"], 4, 16, 12)
        sweep(L1, "1", r["x1"], r["w1"], 5, 15, 10)

        arrive(fine)
        for q in range(5, 15):
            for half in (0, 1):
                r["t0"][q - 5, pl.ds(half, 18, stride=2), :] = r["w1"][q, 0:18]
                r["t0"][q - 5, pl.ds(36 + half, 2, stride=2), :] = r["w1"][q, 30:32]
            for half in (0, 1):
                i = 2 * q - 9 + half
                if q == 5:
                    before = r["lv"][0, half]
                elif q == 14:
                    before = r["lv"][1, half]
                else:
                    before = r["v0"][i]
                r["w0"][i] = before + r["t0"][q - 5]
        sweep(L0, "0", r["w0"], r["x0"], 2, 20, 9)

        def last(i):
            centre, total = spread(L0, "0", r["x0"], i, 8)
            here = pl.ds(i, 8)
            value = (0.3 * centre + r["g0"][here]) + r["inv0"][here] * total
            for k in range(8):
                o_ref[pl.ds(i - 3 + k, 32, stride=16), :] = value[k, 0:32]

        each(3, 19, 8, last)
        for direction in dict.fromkeys(d for d, copy in sent):

            @pl.when(exists(*direction))
            def _():
                for d, copy in sent:
                    if d == direction:
                        copy.wait_send()

        assert serial[0] <= N_MESSAGES

    return kernel


def solution(mesh):
    groups, boxes = mesh.shape["grp"], mesh.shape["box"]

    def body(source, alpha_coef, beta_coef):
        flat = [pltpu.with_memory_space_constraint(v.reshape(512, LANES), pltpu.HBM) for v in (source, alpha_coef, beta_coef)]
        hbm = pl.BlockSpec(memory_space=pltpu.HBM)
        out = pl.pallas_call(
            make_kernel(groups, boxes),
            out_shape=jax.ShapeDtypeStruct((512, LANES), F32),
            in_specs=[hbm, hbm, hbm],
            out_specs=pl.BlockSpec(memory_space=pltpu.VMEM),
            scratch_shapes=[pltpu.VMEM(shape, F32) for shape in SCRATCH.values()]
            + [
                pltpu.SemaphoreType.DMA((3,)),
                pltpu.SemaphoreType.REGULAR,
                pltpu.SemaphoreType.DMA((N_MESSAGES,)),
                pltpu.SemaphoreType.DMA((N_MESSAGES,)),
            ],
            compiler_params=pltpu.CompilerParams(
                collective_id=0, has_side_effects=True, vmem_limit_bytes=48 * 1024 * 1024
            ),
        )(*flat)
        return out.reshape(32, 1, 16, LANES)

    spec = P("grp", "box", None, None)
    return jax.shard_map(body, mesh=mesh, in_specs=(spec, spec, spec), out_specs=spec, check_vma=False)
```
